128 devices in a mesh: grp: 4 (over z), dev: 32 (over y, x, core).
Axes of the slice: x: 4, y: 4, z: 4, core: 2. Of those that a mesh axis runs over, the one named last changes fastest.
Arguments:
- hidden_rows: bfloat16 [1024, 7168], P(('grp', 'dev')), may hold values from -6 to 6
- queries: bfloat16 [1024, 128, 576], P(('grp', 'dev')), may hold values from -320 to 320
- kv_cache: bfloat16 [1024, 512, 576], P(('grp', 'dev')), may hold values from -4 to 4
- cache_lengths: int32 [1024], P(('grp', 'dev')), may hold values from 2 to 512, as said below
- value_lift: bfloat16 [128, 512, 128], P('dev'), may hold values from -0.25 to 0.25
- out_weight: bfloat16 [128, 128, 7168], P('dev'), may hold values from -0.046875 to 0.046875
- expert_ids: int32 [1024, 8], P(('grp', 'dev')), may hold values from 0 to 31, all different within a row; in each aligned block of 4 rows (0 to 3, 4 to 7, ...) at most 2 rows name the same one
- weight_codes: int32 [1024, 8], P(('grp', 'dev')), may hold values from 1 to 255
- w_gate: bfloat16 [32, 7168, 1024], P('dev', None, 'grp'), may hold values from -0.0625 to 0.0625
- w_up: bfloat16 [32, 7168, 1024], P('dev', None, 'grp'), may hold values from -0.0625 to 0.0625
- w_down: bfloat16 [32, 1024, 7168], P('dev', 'grp'), may hold values from -0.1875 to 0.1875
Outputs:
- layer_out: bfloat16 [1024, 7168], P(('grp', 'dev'))
The draws below stay inside these ranges and needn't reach their ends.
Inputs may be any that keep to these rules, and one draw needn't show every extreme that they name: `expert_ids`: each row names 8 different experts; in each aligned block of 4 rows no expert is named by more than 2 rows, and in some block one expert is named by exactly 2. `cache_lengths`: some request has exactly 512 live positions.
All inputs are finite; a program needn't handle non-finite values.
Results may differ from the reference program's by a relative error of at most 0.012.
Values may be sent and summed in bfloat16 or wider, within the bound.
No kernel may reach another device: no remote copies, remote signals or barrier semaphores. Data moves between devices by JAX's collectives and lax.ppermute only.
A program may use at most 128 MiB of HBM per device.

```python
import math
import jax
import jax.numpy as jnp
import numpy as np
from jax import lax

D = 7168
HEADS = 128
LATENT = 512
ROPE = 64
HEAD_V = 128
TOP = 8
MOE_FF = 1024
CACHE = 512
HALF_ROWS = 4
REQUESTS = 1024
EXPERTS = 32
CAP = 2
N_DEV = 32


def plan_lengths(key):
    length_draw = jax.random.randint(jax.random.fold_in(key, 11), (REQUESTS,), 2, CACHE + 1)
    chosen_one = jax.random.randint(jax.random.fold_in(key, 12), (), 0, REQUESTS)
    return jnp.where(jnp.arange(REQUESTS) == chosen_one, CACHE, length_draw).astype(jnp.int32)


def draw_cache_lengths(key, part):
    return plan_lengths(key)


def rotary_keys(key):
    return jnp.clip(jax.random.normal(jax.random.fold_in(key, 22), (REQUESTS, CACHE, ROPE), jnp.float32), -4.0, 4.0)


def draw_kv_cache(key, part):
    latent_draw = jnp.clip(jax.random.normal(jax.random.fold_in(key, 21), (REQUESTS, CACHE, LATENT), jnp.float32), -4.0, 4.0)
    rotary_draw = rotary_keys(key)
    return jnp.concatenate([latent_draw, rotary_draw], axis=2).astype(jnp.bfloat16)


def draw_queries(key, part):
    query_draw = jnp.clip(jax.random.normal(jax.random.fold_in(key, 41), (REQUESTS, HEADS, LATENT + ROPE), jnp.float32), -4.0, 4.0)
    return query_draw.astype(jnp.bfloat16)


def plant(values, rng, low, top_value):
    longest = values.shape.index(max(values.shape))
    spots = []
    for shift in (0, 1):
        where = [jax.random.randint(jax.random.fold_in(rng, axis), (), 0, length) for axis, length in enumerate(values.shape)]
        where[longest] = (where[longest] + shift) % values.shape[longest]
        spots.append(tuple(where))
    return values.at[spots[0]].set(low).at[spots[1]].set(top_value)


def levels(key, extent, pieces, smallest, largest):
    gain, own = 1.0, jax.random.fold_in(key, 6)
    for dim, parts in pieces:
        steps = jnp.exp(jax.random.uniform(jax.random.fold_in(own, dim), (parts,), jnp.float32, smallest / len(pieces), largest / len(pieces)))
        gain = gain * jnp.repeat(steps, extent[dim] // parts).reshape([-1 if axis == dim else 1 for axis in range(len(extent))])
    return gain


def routed_block(stream_key, own, number, rows, amount, top, most, slope):
    ranking = jax.random.permutation(stream_key, amount)
    heavy_load, common = portions_of(amount, rows * top, most, slope, True), portions_of(amount, rows * top, most, slope, False)
    places = jnp.arange(amount)

    def named(tallies, offset_by):
        used = int((tallies > 0).sum())
        fixed = max(1, used // 4)
        passed = fixed + (places - fixed + offset_by * (used - fixed)) % max(1, amount - fixed)
        return jnp.zeros((amount,), jnp.int32).at[ranking[jnp.where(places < fixed, places, passed)]].set(jnp.asarray(tallies, jnp.int32))

    tallies = jnp.where(number % 4 == 0, named(heavy_load, number // 4), named(common, number - number // 4 - 1))
    mixed = jax.random.permutation(jax.random.fold_in(own, 3), amount)
    source_of, receiver = mixed[0:amount // 2 * 2:2], mixed[1:amount // 2 * 2:2]
    margin = jnp.minimum(tallies[source_of] - 1, most - tallies[receiver]) // 2
    margin = jnp.where((source_of == ranking[0]) | (receiver == ranking[0]) | (tallies[receiver] == 0), 0, jnp.maximum(margin, 0))
    passed = jax.random.randint(jax.random.fold_in(own, 4), (amount // 2,), 0, 1 << 20) % (margin + 1)
    tallies = tallies.at[source_of].add(-passed).at[receiver].add(passed)
    labels = jnp.searchsorted(jnp.cumsum(tallies), jnp.arange(rows * top), side="right").astype(jnp.int32)
    grid = labels.reshape(top, rows).T
    grid = grid[jax.random.permutation(jax.random.fold_in(own, 1), rows)]
    offset_by = jax.random.randint(jax.random.fold_in(own, 2), (rows, 1), 0, top)
    return jnp.take_along_axis(grid, (jnp.arange(top)[None, :] + offset_by) % top, axis=1)


def portions_of(count, total, reach, lean, full):
    portions = [(1 << 20) // math.isqrt(grade ** lean) + 1 for grade in range(1, count + 1)]
    largest = reach if full else min(reach, max(-(-total // count), total * portions[0] // sum(portions)))
    least = 1 if total - largest >= count - 1 else 0
    counts, spare = [largest] + [least] * (count - 1), total - largest - least * (count - 1)
    while spare > 0:
        candidates = [i for i in range(1, count) if counts[i] < largest] or [i for i in range(1, count) if counts[i] < reach]
        mass, left = sum([portions[i] for i in candidates]), spare
        for i in candidates:
            extra = min(reach - counts[i], max(1, left * portions[i] // mass), spare)
            counts[i] = counts[i] + extra
            spare = spare - extra
    return np.array(counts)


def normal_values(key, dims, width, bound, split=(), kind=jnp.bfloat16):
    result = jax.random.normal(key, dims, jnp.float32) * width
    if len(split) > 0:
        result = levels(key, dims, split, -0.22, 0.18) * result
    return jnp.clip(result, min=-bound, max=bound).astype(kind)


def setup_inputs(seed: int = 0) -> dict:
    splits = jax.random.split(jax.random.key(seed), 12)
    hidden_rows = normal_values(splits[0], (REQUESTS, D), 1.0, 6.0, ((0, 128),))
    queries = draw_queries(jax.random.fold_in(splits[11], 71), 0)
    kv_cache = draw_kv_cache(jax.random.fold_in(splits[11], 71), 0)
    cache_lengths = draw_cache_lengths(jax.random.fold_in(splits[11], 71), 0)
    value_lift = normal_values(splits[4], (HEADS, LATENT, HEAD_V), LATENT ** -0.5, 0.25, ((0, 32),))
    out_weight = normal_values(splits[5], (HEADS, HEAD_V, D), (HEADS * HEAD_V) ** -0.5, 0.046875, ((0, 32),))
    expert_ids_keys = jax.random.split(jax.random.fold_in(splits[6], 1), REQUESTS // HALF_ROWS)
    expert_ids_turns = jax.random.permutation(jax.random.fold_in(splits[6], 3), REQUESTS // HALF_ROWS)
    expert_ids = jax.vmap(lambda own, number: routed_block(jax.random.fold_in(splits[6], 2), own, number, HALF_ROWS, N_DEV, TOP, CAP, 2))(expert_ids_keys, expert_ids_turns).reshape((REQUESTS, TOP))
    weight_codes = plant(jax.random.randint(splits[7], (REQUESTS, TOP), 1, 256), jax.random.fold_in(splits[7], 1), 1, 255).astype(jnp.int32)
    w_gate = normal_values(splits[8], (EXPERTS, D, MOE_FF), D ** -0.5, 0.0625, ((0, 32), (2, 4)))
    w_up = normal_values(splits[9], (EXPERTS, D, MOE_FF), D ** -0.5, 0.0625, ((0, 32), (2, 4)))
    w_down = normal_values(splits[10], (EXPERTS, MOE_FF, D), MOE_FF ** -0.5, 0.1875, ((0, 32), (1, 4)))
    return dict(hidden_rows=hidden_rows, queries=queries, kv_cache=kv_cache, cache_lengths=cache_lengths, value_lift=value_lift, out_weight=out_weight, expert_ids=expert_ids, weight_codes=weight_codes, w_gate=w_gate, w_up=w_up, w_down=w_down)


score_scale = 192.0 ** (-0.5)

def attend(request_block):
    query_part, cache_part, length_part = request_block
    logits = jnp.einsum('rhk,rck->rhc', query_part.astype(jnp.float32), cache_part.astype(jnp.float32)) * score_scale
    live_mask = jnp.arange(cache_part.shape[1], dtype=jnp.int32)[None, None, :] < length_part[:, None, None]
    logits = jnp.where(live_mask, logits, -jnp.inf)
    highest = lax.optimization_barrier(jnp.max(logits, axis=2, keepdims=True))
    exponent = jnp.exp(logits - highest)
    soft_weights = (exponent / lax.optimization_barrier(jnp.sum(exponent, axis=2, keepdims=True))).astype(jnp.bfloat16)
    latent_part = cache_part[:, :, :LATENT].astype(jnp.float32)
    return jnp.einsum('rhc,rcl->rhl', soft_weights.astype(jnp.float32), latent_part).astype(jnp.bfloat16)

def reference(hidden_rows, queries, kv_cache, cache_lengths, value_lift, out_weight, expert_ids, weight_codes, w_gate, w_up, w_down):
    block_size = math.gcd(REQUESTS, 64)
    block_count = REQUESTS // block_size
    heads_out = lax.map(attend, (queries.reshape(block_count, block_size, HEADS, -1), kv_cache.reshape(block_count, block_size, CACHE, -1), cache_lengths.reshape(block_count, block_size)))
    heads_out = heads_out.reshape(REQUESTS, HEADS, LATENT)
    head_values = jnp.einsum('rhl,hlv->rhv', heads_out.astype(jnp.float32), value_lift.astype(jnp.float32)).astype(jnp.bfloat16)
    attention = jnp.dot(head_values.reshape(REQUESTS, HEADS * HEAD_V), out_weight.reshape(HEADS * HEAD_V, D), preferred_element_type=jnp.float32)
    residual = hidden_rows.astype(jnp.float32) + attention
    normed = (residual * lax.rsqrt(lax.optimization_barrier(jnp.mean(residual * residual, axis=1, keepdims=True)) + 1e-06)).astype(jnp.bfloat16)
    code_values = weight_codes.astype(jnp.float32)
    route_weights = 2.5 * code_values / lax.optimization_barrier(jnp.sum(code_values, axis=1, keepdims=True))

    def expert_step(running, inputs):
        gate_matrix, up_matrix, down_matrix, expert_index = inputs
        gate_part = jnp.dot(normed, gate_matrix, preferred_element_type=jnp.float32)
        up_part = jnp.dot(normed, up_matrix, preferred_element_type=jnp.float32)
        expert_hidden = (jax.nn.silu(gate_part) * up_part).astype(jnp.bfloat16)
        expert_out = jnp.dot(expert_hidden, down_matrix, preferred_element_type=jnp.float32).astype(jnp.bfloat16)
        share_column = lax.optimization_barrier(jnp.sum(jnp.where(expert_ids == expert_index, route_weights, jnp.zeros_like(route_weights)), axis=1))
        return (running + share_column[:, None] * expert_out.astype(jnp.float32), None)
    start_value = jnp.zeros((REQUESTS, D), jnp.float32)
    combined, _ = lax.scan(expert_step, start_value, (w_gate, w_up, w_down, jnp.arange(EXPERTS, dtype=jnp.int32)))
    return (residual + combined).astype(jnp.bfloat16)
```

```python
import jax
import jax.numpy as jnp
from jax import lax
from jax.sharding import PartitionSpec as P

LATENT = 512
SCALE = 192.0 ** (-0.5)
ALL = ("grp", "dev")
BF = jnp.bfloat16
F32 = jnp.float32


def place(i):
    return [i // 32, (i // 8) % 4, (i // 2) % 4, i % 2]


def number(at):
    return ((at[0] * 4 + at[1]) * 4 + at[2]) * 2 + at[3]


def core_pairs():
    return [(i, i ^ 1) for i in range(128)]


def ring_pairs(axis, step):
    pairs = []
    for i in range(128):
        at = place(i)
        flip = (1, 3) if at[3] == 0 else (3, 1)
        at[axis] ^= flip[step]
        pairs.append((i, number(at)))
    return pairs


Z, Y, X = 0, 1, 2


def swap(value, axis, step):
    return lax.ppermute(value, ALL, ring_pairs(axis, step))


def other_core(value):
    return lax.ppermute(value, ALL, core_pairs())


def attend(queries, kv_cache, cache_lengths):
    logits = jnp.einsum("rhk,rck->rhc", queries, kv_cache, preferred_element_type=F32) * SCALE
    live = lax.broadcasted_iota(jnp.int32, logits.shape, 2) < cache_lengths[:, None, None]
    logits = jnp.where(live, logits, -jnp.inf)
    highest = jnp.max(logits, axis=2, keepdims=True)
    exponent = jnp.exp(logits - highest)
    soft = (exponent / jnp.sum(exponent, axis=2, keepdims=True)).astype(BF)
    return jnp.einsum(
        "rhc,rcl->rhl", soft, kv_cache[:, :, :LATENT], preferred_element_type=F32
    ).astype(BF)


def ring_offset(bits, core):
    low, high = bits % 2, bits // 2
    first = jnp.where(core == 0, 1, 3)
    second = jnp.where(core == 0, 3, 1)
    return (low * first) ^ (high * second)


def plane_order(rows, here, core):
    count = rows // 16
    at = jnp.arange(rows, dtype=jnp.int32)
    block = at // count
    y = (here // 4) ^ ring_offset(block // 4, core)
    x = (here % 4) ^ ring_offset(block % 4, core)
    source = (y * 4 + x) * count + at % count
    return (source[:, None] == jnp.arange(rows, dtype=jnp.int32)[None, :]).astype(BF)


def halves(value):
    half = value.shape[0] // 2
    return value[:half], value[half:]


def fold(value, axis, step):
    keep, send = halves(value)
    got = swap(send, axis, step)
    return (keep.astype(F32) + got.astype(F32)).astype(BF)


def grow(value, axis, step):
    return jnp.concatenate([value, swap(value, axis, step)], axis=0)


def on_device(
    hidden_rows,
    queries,
    kv_cache,
    cache_lengths,
    value_lift,
    out_weight,
    expert_ids,
    weight_codes,
    w_gate,
    w_up,
    w_down,
):
    device = lax.axis_index("dev")
    core = device % 2
    here = device // 2
    rows, width = hidden_rows.shape
    half = width // 2

    lift_other = other_core(value_lift)
    out_other = other_core(out_weight)
    gate_other = other_core(w_gate[0])
    up_other = other_core(w_up[0])
    down_other = other_core(w_down[0])

    heads_out = attend(queries, kv_cache, cache_lengths)
    same_core = [[c + 2 * i for i in range(16)] for c in range(2)]
    moved = lax.all_to_all(
        heads_out, "dev", split_axis=1, concat_axis=0, tiled=True, axis_index_groups=same_core
    )
    all_rows = moved.shape[0]
    own = lax.dynamic_slice_in_dim(moved, 4 * core, 4, 1)
    other = lax.dynamic_slice_in_dim(moved, 4 * (1 - core), 4, 1)

    def lifted(part, lift):
        return jnp.einsum("rhl,hlv->rhv", part, lift, preferred_element_type=F32).astype(BF)

    head_values = jnp.concatenate(
        [lifted(own, value_lift), lifted(other, lift_other)], axis=1
    ).reshape(all_rows, -1)
    order = plane_order(all_rows, here, core)
    head_values = jnp.dot(order, head_values, preferred_element_type=F32).astype(BF)
    depth = head_values.shape[1] // 2
    own_matrix = out_weight.reshape(-1, width)
    other_matrix = out_other.reshape(-1, width)

    def projected(columns):
        return (
            jnp.dot(head_values[:, :depth], own_matrix[:, columns], preferred_element_type=F32)
            + jnp.dot(head_values[:, depth:], other_matrix[:, columns], preferred_element_type=F32)
        ).astype(BF)

    left = projected(slice(0, half))
    right = projected(slice(half, width))
    right = right.reshape(4, 4, rows, half).swapaxes(0, 1).reshape(all_rows, half)
    for axis_left, axis_right, step in ((Y, X, 1), (Y, X, 0), (X, Y, 1), (X, Y, 0)):
        left = fold(left, axis_left, step)
        right = fold(right, axis_right, step)
    attention = jnp.concatenate([left, right], axis=1).astype(F32)
    residual = hidden_rows.astype(F32) + attention
    normed = (
        residual * lax.rsqrt(jnp.mean(residual * residual, axis=1, keepdims=True) + 1e-06)
    ).astype(BF)

    routing = jnp.concatenate([expert_ids, weight_codes], axis=1).astype(BF)
    routing = jnp.pad(routing, ((0, 0), (0, 128 - routing.shape[1])))
    first = grow(jnp.concatenate([normed, routing], axis=1), Z, 0)
    second = swap(first, Z, 1)
    for axis_first, axis_second, step in ((X, Y, 0), (X, Y, 1), (Y, X, 0)):
        first = grow(first, axis_first, step)
        second = grow(second, axis_second, step)
    first_far = swap(first, Y, 1)
    second_far = swap(second, X, 1)

    def expert(rows_in, share, gate, up):
        gate_part = jnp.dot(rows_in, gate, preferred_element_type=F32)
        up_part = jnp.dot(rows_in, up, preferred_element_type=F32)
        return (jax.nn.silu(gate_part) * up_part * share).astype(BF)

    def layer(pieces):
        rows_in = jnp.concatenate([p[:, :width] for p in pieces], axis=0)
        table = jnp.concatenate([p[:, width : width + 16] for p in pieces], axis=0).astype(F32)
        ids, codes = table[:, :8], table[:, 8:]
        weights = 2.5 * codes / jnp.sum(codes, axis=1, keepdims=True)

        def share(number):
            return jnp.sum(
                jnp.where(ids == number.astype(F32), weights, 0.0), axis=1, keepdims=True
            )

        hidden_own = expert(rows_in, share(device), w_gate[0], w_up[0])
        hidden_other = expert(rows_in, share(device ^ 1), gate_other, up_other)
        result = (
            jnp.dot(hidden_own, w_down[0], preferred_element_type=F32)
            + jnp.dot(hidden_other, down_other, preferred_element_type=F32)
        ).astype(BF)
        return halves(result)

    out_first_far, out_second_far = layer([first_far, second_far])
    out_first, out_second = layer([first, second])

    def add(one, two):
        return (one.astype(F32) + two.astype(F32)).astype(BF)

    out_first = add(out_first, swap(out_first_far, Y, 1))
    out_second = add(out_second, swap(out_second_far, X, 1))
    for axis_first, axis_second, step in ((Y, X, 0), (X, Y, 1), (X, Y, 0)):
        out_first = fold(out_first, axis_first, step)
        out_second = fold(out_second, axis_second, step)
    combined = add(out_first, swap(out_second, Z, 1))
    keep, send = halves(combined)
    combined = keep.astype(F32) + swap(send, Z, 0).astype(F32)
    return (residual + combined).astype(BF)


def solution(mesh):
    both = P(ALL, None)
    in_specs = (
        both,
        P(ALL, None, None),
        P(ALL, None, None),
        P(ALL),
        P("dev", None, None),
        P("dev", None, None),
        both,
        both,
        P("dev", None, "grp"),
        P("dev", None, "grp"),
        P("dev", "grp", None),
    )
    return jax.shard_map(
        on_device, mesh=mesh, in_specs=in_specs, out_specs=both, check_vma=False
    )
```

```python
import jax
import jax.numpy as jnp
from jax import lax
from jax.experimental import pallas as pl
from jax.experimental.pallas import tpu as pltpu
from jax.sharding import PartitionSpec as P


LATENT = 512
SCALE = 192.0 ** (-0.5)
ALL = ("grp", "dev")
BF = jnp.bfloat16
F32 = jnp.float32


def place(i):
    return [i // 32, (i // 8) % 4, (i // 2) % 4, i % 2]


def number(at):
    return ((at[0] * 4 + at[1]) * 4 + at[2]) * 2 + at[3]


def core_pairs():
    return [(i, i ^ 1) for i in range(128)]


def ring_pairs(axis, step):
    pairs = []
    for i in range(128):
        at = place(i)
        flip = (1, 3) if at[3] == 0 else (3, 1)
        at[axis] ^= flip[step]
        pairs.append((i, number(at)))
    return pairs


Z, Y, X = 0, 1, 2


def swap(value, axis, step):
    return lax.ppermute(value, ALL, ring_pairs(axis, step))


def other_core(value):
    return lax.ppermute(value, ALL, core_pairs())


PER_STEP = 2


def attend_kernel(length_ref, q_ref, kv_ref, out_ref):
    for j in range(PER_STEP):
        kv = kv_ref[j]
        logits = lax.dot_general(
            q_ref[j], kv, (((0,), (0,)), ((), ())), preferred_element_type=F32
        ) * SCALE
        live = lax.broadcasted_iota(jnp.int32, logits.shape, 1) < length_ref[
            pl.program_id(0) * PER_STEP + j
        ]
        logits = jnp.where(live, logits, -jnp.inf)
        exponent = jnp.exp(logits - jnp.max(logits, axis=1, keepdims=True))
        soft = (exponent / jnp.sum(exponent, axis=1, keepdims=True)).astype(BF)
        result = lax.dot_general(
            soft, kv[:LATENT], (((1,), (1,)), ((), ())), preferred_element_type=F32
        )
        out_ref[:, j] = result.astype(BF).reshape(out_ref.shape[0], out_ref.shape[2], LATENT)


def attend(queries, kv_cache, cache_lengths):
    rows, heads, depth = queries.shape
    live = kv_cache.shape[1]
    return pl.pallas_call(
        attend_kernel,
        grid_spec=pltpu.PrefetchScalarGridSpec(
            num_scalar_prefetch=1,
            grid=(rows // PER_STEP,),
            in_specs=[
                pl.BlockSpec((PER_STEP, depth, heads), lambda i, n: (i, 0, 0)),
                pl.BlockSpec((PER_STEP, depth, live), lambda i, n: (i, 0, 0)),
            ],
            out_specs=pl.BlockSpec((16, PER_STEP, heads // 16, LATENT), lambda i, n: (0, i, 0, 0)),
        ),
        out_shape=jax.ShapeDtypeStruct((16, rows, heads // 16, LATENT), BF),
        name="attend",
    )(cache_lengths, jnp.swapaxes(queries, 1, 2), jnp.swapaxes(kv_cache, 1, 2))


def project_kernel(steps, left_in, right_in, own_ref, other_ref, left_ref, right_ref):
    depth = own_ref.shape[0]

    def run(rows_ref, out_ref):
        out_ref[...] = (
            jnp.dot(rows_ref[:, :depth], own_ref[...], preferred_element_type=F32)
            + jnp.dot(rows_ref[:, depth:], other_ref[...], preferred_element_type=F32)
        ).astype(BF)

    @pl.when(pl.program_id(0) < steps)
    def _():
        run(left_in, left_ref)

    @pl.when(pl.program_id(0) >= steps)
    def _():
        run(right_in, right_ref)


def project(left_in, right_in, own, other):
    rows, depth = left_in.shape
    width = own.shape[1]
    block = 896
    steps = width // 2 // block
    whole = pl.BlockSpec((rows, depth), lambda i: (0, 0))
    matrix = pl.BlockSpec((depth // 2, block), lambda i: (0, i))
    shape = jax.ShapeDtypeStruct((rows, width // 2), BF)
    return pl.pallas_call(
        lambda *refs: project_kernel(steps, *refs),
        grid=(2 * steps,),
        in_specs=[whole, whole, matrix, matrix],
        out_specs=[
            pl.BlockSpec((rows, block), lambda i: (0, jnp.minimum(i, steps - 1))),
            pl.BlockSpec((rows, block), lambda i: (0, jnp.maximum(i - steps, 0))),
        ],
        out_shape=[shape, shape],
        name="project",
    )(left_in, right_in, own, other)


BLOCK = 1024


def experts_kernel(
    steps, number_ref, xa, xb, ra, rb, gate_own, gate_other, up_own, up_other,
    down_own, down_other, out_a, out_b, acc, hidden,
):
    step = pl.program_id(0)
    units = gate_own.shape[1]

    @pl.when(step == 0)
    def _():
        acc[...] = jnp.zeros_like(acc)

    @pl.when(step < steps)
    def _():
        rows = jnp.concatenate([xa[...], xb[...]], axis=0)
        for at, matrix in enumerate((gate_own, up_own, gate_other, up_other)):
            acc[:, at * units : (at + 1) * units] += jnp.dot(
                rows, matrix[...], preferred_element_type=F32
            )

    @pl.when(step == steps - 1)
    def _():
        table = jnp.concatenate([ra[...], rb[...]], axis=0).astype(F32)
        ids, codes = table[:, :8], table[:, 8:16]
        weights = 2.5 * codes / jnp.sum(codes, axis=1, keepdims=True)
        for at in range(2):
            named = ids == (number_ref[at]).astype(F32)
            share = jnp.sum(jnp.where(named, weights, 0.0), axis=1, keepdims=True)
            gate = acc[:, 2 * at * units : (2 * at + 1) * units]
            up = acc[:, (2 * at + 1) * units : (2 * at + 2) * units]
            value = gate / (1.0 + jnp.exp(-gate)) * up * share
            hidden[:, at * units : (at + 1) * units] = value.astype(BF)

    @pl.when(step >= steps)
    def _():
        result = jnp.dot(
            hidden[:, :units], down_own[...], preferred_element_type=F32
        ) + jnp.dot(hidden[:, units:], down_other[...], preferred_element_type=F32)
        half = result.shape[0] // 2
        out_a[...] = result[:half].astype(BF)
        out_b[...] = result[half:].astype(BF)


def experts(numbers, xa, xb, weights, width):
    rows = xa.shape[0]
    units = weights[0].shape[2]
    steps = width // BLOCK
    first = lambda i, n: (0, jnp.minimum(i, steps - 1))
    routing = pl.BlockSpec((rows, 128), lambda i, n: (0, width // 128))
    into = pl.BlockSpec(
        (pl.Squeezed(), BLOCK, units), lambda i, n: (0, jnp.minimum(i, steps - 1), 0)
    )
    onward = pl.BlockSpec(
        (pl.Squeezed(), units, BLOCK), lambda i, n: (0, 0, jnp.maximum(i - steps, 0))
    )
    back = pl.BlockSpec((rows, BLOCK), lambda i, n: (0, jnp.maximum(i - steps, 0)))
    shape = jax.ShapeDtypeStruct((rows, width), BF)
    return pl.pallas_call(
        lambda *refs: experts_kernel(steps, *refs),
        grid_spec=pltpu.PrefetchScalarGridSpec(
            num_scalar_prefetch=1,
            grid=(2 * steps,),
            in_specs=[
                pl.BlockSpec((rows, BLOCK), first),
                pl.BlockSpec((rows, BLOCK), first),
                routing,
                routing,
                into,
                into,
                into,
                into,
                onward,
                onward,
            ],
            out_specs=[back, back],
            scratch_shapes=[
                pltpu.VMEM((2 * rows, 4 * units), F32),
                pltpu.VMEM((2 * rows, 2 * units), BF),
            ],
        ),
        out_shape=[shape, shape],
        name="experts",
    )(numbers, xa, xb, xa, xb, *weights)


def ring_offset(bits, core):
    low, high = bits % 2, bits // 2
    first = jnp.where(core == 0, 1, 3)
    second = jnp.where(core == 0, 3, 1)
    return (low * first) ^ (high * second)


def plane_order(rows, here, core, y_first):
    count = rows // 16
    at = jnp.arange(rows, dtype=jnp.int32)
    block = at // count
    major, minor = block // 4, block % 4
    y = (here // 4) ^ ring_offset(major if y_first else minor, core)
    x = (here % 4) ^ ring_offset(minor if y_first else major, core)
    source = (y * 4 + x) * count + at % count
    return (source[:, None] == jnp.arange(rows, dtype=jnp.int32)[None, :]).astype(BF)


def halves(value):
    half = value.shape[0] // 2
    return value[:half], value[half:]


def fold(value, axis, step):
    keep, send = halves(value)
    got = swap(send, axis, step)
    return (keep.astype(F32) + got.astype(F32)).astype(BF)


def grow(value, axis, step):
    return jnp.concatenate([value, swap(value, axis, step)], axis=0)


def run_rows(
    hidden_rows,
    queries,
    kv_cache,
    cache_lengths,
    value_lift,
    out_weight,
    expert_ids,
    weight_codes,
    w_gate,
    w_up,
    w_down,
):
    device = lax.axis_index("dev")
    core = device % 2
    here = device // 2
    _, width = hidden_rows.shape

    swapped = []
    for matrix in (value_lift, out_weight, w_gate, w_up, w_down):
        swapped.append(other_core(matrix))
    lift_other, out_other, gate_other, up_other, down_other = swapped

    heads_out = attend(queries, kv_cache, cache_lengths)
    same_core = [[c + 2 * i for i in range(16)] for c in range(2)]
    moved = lax.all_to_all(
        heads_out, "dev", split_axis=0, concat_axis=0, tiled=True, axis_index_groups=same_core
    )
    all_rows = moved.shape[0] * moved.shape[1]
    moved = moved.reshape(all_rows, moved.shape[2], LATENT)
    own = lax.dynamic_slice_in_dim(moved, 4 * core, 4, 1)
    other = lax.dynamic_slice_in_dim(moved, 4 * (1 - core), 4, 1)

    def lifted(part, lift):
        return jnp.einsum("rhl,hlv->rhv", part, lift, preferred_element_type=F32).astype(BF)

    head_values = jnp.concatenate(
        [lifted(own, value_lift), lifted(other, lift_other)], axis=1
    ).reshape(all_rows, -1)

    def ordered(y_first):
        order = plane_order(all_rows, here, core, y_first)
        return jnp.dot(order, head_values, preferred_element_type=F32).astype(BF)

    left, right = project(
        ordered(True),
        ordered(False),
        out_weight.reshape(-1, width),
        out_other.reshape(-1, width),
    )
    for axis_left, axis_right, step in ((Y, X, 1), (Y, X, 0), (X, Y, 1), (X, Y, 0)):
        left = fold(left, axis_left, step)
        right = fold(right, axis_right, step)
    attention = jnp.concatenate([left, right], axis=1).astype(F32)
    residual = hidden_rows.astype(F32) + attention
    normed = (
        residual * lax.rsqrt(jnp.mean(residual * residual, axis=1, keepdims=True) + 1e-06)
    ).astype(BF)

    routing = jnp.concatenate([expert_ids, weight_codes], axis=1).astype(BF)
    routing = jnp.pad(routing, ((0, 0), (0, 128 - routing.shape[1])))
    first = grow(jnp.concatenate([normed, routing], axis=1), Z, 0)
    second = swap(first, Z, 1)
    for axis_first, axis_second, step in ((X, Y, 0), (X, Y, 1), (Y, X, 0)):
        first = grow(first, axis_first, step)
        second = grow(second, axis_second, step)
    first_far = swap(first, Y, 1)
    second_far = swap(second, X, 1)

    numbers = jnp.stack([device, device ^ 1]).astype(jnp.int32)
    weights = (w_gate, gate_other, w_up, up_other, w_down, down_other)
    out_first, out_second = experts(numbers, first, second, weights, width)
    out_first_far, out_second_far = experts(numbers, first_far, second_far, weights, width)

    def add(one, two):
        return (one.astype(F32) + two.astype(F32)).astype(BF)

    out_first = add(out_first, swap(out_first_far, Y, 1))
    out_second = add(out_second, swap(out_second_far, X, 1))
    for axis_first, axis_second, step in ((Y, X, 0), (X, Y, 1), (X, Y, 0)):
        out_first = fold(out_first, axis_first, step)
        out_second = fold(out_second, axis_second, step)
    combined = add(out_first, swap(out_second, Z, 1))
    keep, send = halves(combined)
    combined = keep.astype(F32) + swap(send, Z, 0).astype(F32)
    return (residual + combined).astype(BF)


def solution(mesh):
    both = P(ALL, None)
    in_specs = (
        both,
        P(ALL, None, None),
        P(ALL, None, None),
        P(ALL),
        P("dev", None, None),
        P("dev", None, None),
        both,
        both,
        P("dev", None, "grp"),
        P("dev", None, "grp"),
        P("dev", "grp", None),
    )
    return jax.shard_map(run_rows, mesh=mesh, in_specs=in_specs, out_specs=both, check_vma=False)
```

```python
import jax
import jax.numpy as jnp
from jax import lax
from jax.experimental import pallas as pl
from jax.experimental.pallas import tpu as pltpu
from jax.sharding import PartitionSpec as P


LATENT = 512
SCALE = 192.0 ** (-0.5)
ALL = ("grp", "dev")
BF = jnp.bfloat16
F32 = jnp.float32


def place(i):
    return [i // 32, (i // 8) % 4, (i // 2) % 4, i % 2]


def number(at):
    return ((at[0] * 4 + at[1]) * 4 + at[2]) * 2 + at[3]


def core_pairs():
    return [(i, i ^ 1) for i in range(128)]


def ring_pairs(axis, step):
    pairs = []
    for i in range(128):
        at = place(i)
        flip = (1, 3) if at[3] == 0 else (3, 1)
        at[axis] ^= flip[step]
        pairs.append((i, number(at)))
    return pairs


def ring_next(axis):
    pairs = []
    for i in range(128):
        at = place(i)
        at[axis] = (at[axis] + (1 if at[3] == 0 else 3)) % 4
        pairs.append((i, number(at)))
    return pairs


Z, Y, X = 0, 1, 2


def swap(value, axis, step):
    return lax.ppermute(value, ALL, ring_pairs(axis, step))


def onward(value, axis):
    return lax.ppermute(value, ALL, ring_next(axis))


def other_core(value):
    return lax.ppermute(value, ALL, core_pairs())


PER_STEP = 2


def attend_kernel(length_ref, q_ref, kv_ref, out_ref):
    for j in range(PER_STEP):
        kv = kv_ref[j]
        logits = lax.dot_general(
            q_ref[j], kv, (((0,), (0,)), ((), ())), preferred_element_type=F32
        ) * SCALE
        live = lax.broadcasted_iota(jnp.int32, logits.shape, 1) < length_ref[
            pl.program_id(0) * PER_STEP + j
        ]
        logits = jnp.where(live, logits, -jnp.inf)
        exponent = jnp.exp(logits - jnp.max(logits, axis=1, keepdims=True))
        soft = (exponent / jnp.sum(exponent, axis=1, keepdims=True)).astype(BF)
        result = lax.dot_general(
            soft, kv[:LATENT], (((1,), (1,)), ((), ())), preferred_element_type=F32
        )
        out_ref[:, j] = result.astype(BF).reshape(out_ref.shape[0], out_ref.shape[2], LATENT)


def attend(queries, kv_cache, cache_lengths):
    rows, heads, depth = queries.shape
    live = kv_cache.shape[1]
    return pl.pallas_call(
        attend_kernel,
        grid_spec=pltpu.PrefetchScalarGridSpec(
            num_scalar_prefetch=1,
            grid=(rows // PER_STEP,),
            in_specs=[
                pl.BlockSpec((PER_STEP, depth, heads), lambda i, n: (i, 0, 0)),
                pl.BlockSpec((PER_STEP, depth, live), lambda i, n: (i, 0, 0)),
            ],
            out_specs=pl.BlockSpec((16, PER_STEP, heads // 16, LATENT), lambda i, n: (0, i, 0, 0)),
        ),
        out_shape=jax.ShapeDtypeStruct((16, rows, heads // 16, LATENT), BF),
        name="attend",
    )(cache_lengths, jnp.swapaxes(queries, 1, 2), jnp.swapaxes(kv_cache, 1, 2))


def project_kernel(steps, left_in, right_in, own_ref, other_ref, left_ref, right_ref):
    depth = own_ref.shape[0]

    def run(rows_ref, out_ref):
        out_ref[...] = (
            jnp.dot(rows_ref[:, :depth], own_ref[...], preferred_element_type=F32)
            + jnp.dot(rows_ref[:, depth:], other_ref[...], preferred_element_type=F32)
        ).astype(BF)

    @pl.when(pl.program_id(0) < steps)
    def _():
        run(left_in, left_ref)

    @pl.when(pl.program_id(0) >= steps)
    def _():
        run(right_in, right_ref)


def project(left_in, right_in, own, other):
    rows, depth = left_in.shape
    width = own.shape[1]
    block = 1792
    steps = width // 2 // block
    whole = pl.BlockSpec((rows, depth), lambda i: (0, 0))
    matrix = pl.BlockSpec((depth // 2, block), lambda i: (0, i))
    shape = jax.ShapeDtypeStruct((rows, width // 2), BF)
    return pl.pallas_call(
        lambda *refs: project_kernel(steps, *refs),
        grid=(2 * steps,),
        in_specs=[whole, whole, matrix, matrix],
        out_specs=[
            pl.BlockSpec((rows, block), lambda i: (0, jnp.minimum(i, steps - 1))),
            pl.BlockSpec((rows, block), lambda i: (0, jnp.maximum(i - steps, 0))),
        ],
        out_shape=[shape, shape],
        name="project",
    )(left_in, right_in, own, other)


BLOCK = 1792


def experts_kernel(
    steps, number_ref, xa, xb, ra, rb, gate_own, gate_other, up_own, up_other,
    down_own, down_other, out_a, out_b, acc, hidden,
):
    step = pl.program_id(0)
    units = gate_own.shape[1]

    @pl.when(step == 0)
    def _():
        acc[...] = jnp.zeros_like(acc)

    @pl.when(step < steps)
    def _():
        rows = jnp.concatenate([xa[...], xb[...]], axis=0)
        for at, matrix in enumerate((gate_own, up_own, gate_other, up_other)):
            acc[:, at * units : (at + 1) * units] += jnp.dot(
                rows, matrix[...], preferred_element_type=F32
            )

    @pl.when(step == steps - 1)
    def _():
        table = jnp.concatenate([ra[...], rb[...]], axis=0).astype(F32)
        ids, codes = table[:, :8], table[:, 8:16]
        weights = 2.5 * codes / jnp.sum(codes, axis=1, keepdims=True)
        for at in range(2):
            named = ids == (number_ref[at]).astype(F32)
            share = jnp.sum(jnp.where(named, weights, 0.0), axis=1, keepdims=True)
            gate = acc[:, 2 * at * units : (2 * at + 1) * units]
            up = acc[:, (2 * at + 1) * units : (2 * at + 2) * units]
            value = gate / (1.0 + jnp.exp(-gate)) * up * share
            hidden[:, at * units : (at + 1) * units] = value.astype(BF)

    @pl.when(step >= steps)
    def _():
        result = jnp.dot(
            hidden[:, :units], down_own[...], preferred_element_type=F32
        ) + jnp.dot(hidden[:, units:], down_other[...], preferred_element_type=F32)
        half = result.shape[0] // 2
        out_a[...] = result[:half].astype(BF)
        out_b[...] = result[half:].astype(BF)


def experts(numbers, xa, xb, weights, width):
    rows = xa.shape[0]
    units = weights[0].shape[2]
    steps = width // BLOCK
    first = lambda i, n: (0, jnp.minimum(i, steps - 1))
    routing = pl.BlockSpec((rows, 128), lambda i, n: (0, width // 128))
    into = pl.BlockSpec(
        (pl.Squeezed(), BLOCK, units), lambda i, n: (0, jnp.minimum(i, steps - 1), 0)
    )
    onward = pl.BlockSpec(
        (pl.Squeezed(), units, BLOCK), lambda i, n: (0, 0, jnp.maximum(i - steps, 0))
    )
    back = pl.BlockSpec((rows, BLOCK), lambda i, n: (0, jnp.maximum(i - steps, 0)))
    shape = jax.ShapeDtypeStruct((rows, width), BF)
    return pl.pallas_call(
        lambda *refs: experts_kernel(steps, *refs),
        grid_spec=pltpu.PrefetchScalarGridSpec(
            num_scalar_prefetch=1,
            grid=(2 * steps,),
            in_specs=[
                pl.BlockSpec((rows, BLOCK), first),
                pl.BlockSpec((rows, BLOCK), first),
                routing,
                routing,
                into,
                into,
                into,
                into,
                onward,
                onward,
            ],
            out_specs=[back, back],
            scratch_shapes=[
                pltpu.VMEM((2 * rows, 4 * units), F32),
                pltpu.VMEM((2 * rows, 2 * units), BF),
            ],
        ),
        out_shape=[shape, shape],
        name="experts",
    )(numbers, xa, xb, xa, xb, *weights)


def ring_offset(bits, core):
    low, high = bits % 2, bits // 2
    first = jnp.where(core == 0, 1, 3)
    second = jnp.where(core == 0, 3, 1)
    return (low * first) ^ (high * second)


def plane_order(rows, here, core, y_first):
    count = rows // 16
    at = jnp.arange(rows, dtype=jnp.int32)
    block = at // count
    major, minor = block // 4, block % 4
    y = (here // 4) ^ ring_offset(major if y_first else minor, core)
    x = (here % 4) ^ ring_offset(minor if y_first else major, core)
    source = (y * 4 + x) * count + at % count
    return (source[:, None] == jnp.arange(rows, dtype=jnp.int32)[None, :]).astype(BF)


def halves(value):
    half = value.shape[0] // 2
    return value[:half], value[half:]


def fold(value, axis, step):
    keep, send = halves(value)
    got = swap(send, axis, step)
    return (keep.astype(F32) + got.astype(F32)).astype(BF)


def grow(value, axis, step):
    return jnp.concatenate([value, swap(value, axis, step)], axis=0)


def run_rows(
    hidden_rows,
    queries,
    kv_cache,
    cache_lengths,
    value_lift,
    out_weight,
    expert_ids,
    weight_codes,
    w_gate,
    w_up,
    w_down,
):
    device = lax.axis_index("dev")
    core = device % 2
    here = device // 2
    _, width = hidden_rows.shape

    swapped = []
    for matrix in (value_lift, out_weight, w_gate, w_up, w_down):
        swapped.append(other_core(matrix))
    lift_other, out_other, gate_other, up_other, down_other = swapped

    heads_out = attend(queries, kv_cache, cache_lengths)
    same_core = [[c + 2 * i for i in range(16)] for c in range(2)]
    moved = lax.all_to_all(
        heads_out, "dev", split_axis=0, concat_axis=0, tiled=True, axis_index_groups=same_core
    )
    all_rows = moved.shape[0] * moved.shape[1]
    moved = moved.reshape(all_rows, moved.shape[2], LATENT)
    own = lax.dynamic_slice_in_dim(moved, 4 * core, 4, 1)
    other = lax.dynamic_slice_in_dim(moved, 4 * (1 - core), 4, 1)

    def lifted(part, lift):
        return jnp.einsum("rhl,hlv->rhv", part, lift, preferred_element_type=F32).astype(BF)

    head_values = jnp.concatenate(
        [lifted(own, value_lift), lifted(other, lift_other)], axis=1
    ).reshape(all_rows, -1)

    def ordered(y_first):
        order = plane_order(all_rows, here, core, y_first)
        return jnp.dot(order, head_values, preferred_element_type=F32).astype(BF)

    left, right = project(
        ordered(True),
        ordered(False),
        out_weight.reshape(-1, width),
        out_other.reshape(-1, width),
    )
    for axis_left, axis_right, step in ((Y, X, 1), (Y, X, 0), (X, Y, 1), (X, Y, 0)):
        left = fold(left, axis_left, step)
        right = fold(right, axis_right, step)
    attention = jnp.concatenate([left, right], axis=1).astype(F32)
    residual = hidden_rows.astype(F32) + attention
    normed = (
        residual * lax.rsqrt(jnp.mean(residual * residual, axis=1, keepdims=True) + 1e-06)
    ).astype(BF)

    routing = jnp.concatenate([expert_ids, weight_codes], axis=1).astype(BF)
    routing = jnp.pad(routing, ((0, 0), (0, 128 - routing.shape[1])))
    first = grow(jnp.concatenate([normed, routing], axis=1), Z, 0)
    second = swap(first, Z, 1)
    for step in range(2):
        first = grow(first, X, step)
        second = grow(second, Y, step)

    def add(one, two):
        return (one.astype(F32) + two.astype(F32)).astype(BF)

    numbers = jnp.stack([device, device ^ 1]).astype(jnp.int32)
    weights = (w_gate, gate_other, w_up, up_other, w_down, down_other)
    held = [(first, second)]
    for _ in range(1, 4):
        one = onward(held[-1][0], Y)
        two = onward(held[-1][1], X)
        held.append((one, two))
    done = []
    for hop in range(4):
        done.append(experts(numbers, *held[hop], weights, width))
    one, two = done[1]
    for hop in range(1, 4):
        one = onward(one, Y)
        two = onward(two, X)
        one = add(one, done[(hop + 1) % 4][0])
        two = add(two, done[(hop + 1) % 4][1])
    for step in (1, 0):
        one = fold(one, X, step)
        two = fold(two, Y, step)
    combined = add(one, swap(two, Z, 1))
    keep, send = halves(combined)
    combined = keep.astype(F32) + swap(send, Z, 0).astype(F32)
    return (residual + combined).astype(BF)


def solution(mesh):
    both = P(ALL, None)
    in_specs = (
        both,
        P(ALL, None, None),
        P(ALL, None, None),
        P(ALL),
        P("dev", None, None),
        P("dev", None, None),
        both,
        both,
        P("dev", None, "grp"),
        P("dev", None, "grp"),
        P("dev", "grp", None),
    )
    return jax.shard_map(
        run_rows, mesh=mesh, in_specs=in_specs, out_specs=both, check_vma=False
    )
```

```python
import jax
import jax.numpy as jnp
from jax import lax
from jax.experimental import pallas as pl
from jax.experimental.pallas import tpu as pltpu
from jax.sharding import PartitionSpec as P


LATENT = 512
SCALE = 192.0 ** (-0.5)
ALL = ("grp", "dev")
BF = jnp.bfloat16
F32 = jnp.float32


def place(i):
    return [i // 32, (i // 8) % 4, (i // 2) % 4, i % 2]


def number(at):
    return ((at[0] * 4 + at[1]) * 4 + at[2]) * 2 + at[3]


def core_pairs():
    return [(i, i ^ 1) for i in range(128)]


def ring_pairs(axis, step):
    pairs = []
    for i in range(128):
        at = place(i)
        flip = (1, 3) if at[3] == 0 else (3, 1)
        at[axis] ^= flip[step]
        pairs.append((i, number(at)))
    return pairs


def ring_next(axis, hops=1):
    pairs = []
    for i in range(128):
        at = place(i)
        at[axis] = (at[axis] + (hops if at[3] == 0 else 4 - hops)) % 4
        pairs.append((i, number(at)))
    return pairs


Z, Y, X = 0, 1, 2


def swap(value, axis, step):
    return lax.ppermute(value, ALL, ring_pairs(axis, step))


def onward(value, axis, hops=1):
    return lax.ppermute(value, ALL, ring_next(axis, hops))


def other_core(value):
    return lax.ppermute(value, ALL, core_pairs())


PER_STEP = 2
PARTS = 1


def attend_kernel(first, length_ref, q_ref, kv_ref, out_ref):
    for j in range(PER_STEP):
        kv = kv_ref[j]
        logits = lax.dot_general(
            q_ref[j], kv, (((0,), (0,)), ((), ())), preferred_element_type=F32
        ) * SCALE
        live = lax.broadcasted_iota(jnp.int32, logits.shape, 1) < length_ref[
            first + pl.program_id(0) * PER_STEP + j
        ]
        logits = jnp.where(live, logits, -jnp.inf)
        exponent = jnp.exp(logits - jnp.max(logits, axis=1, keepdims=True))
        soft = (exponent / jnp.sum(exponent, axis=1, keepdims=True)).astype(BF)
        result = lax.dot_general(
            soft, kv[:LATENT], (((1,), (1,)), ((), ())), preferred_element_type=F32
        )
        out_ref[:, j] = result.astype(BF).reshape(out_ref.shape[0], out_ref.shape[2], LATENT)


def attend(queries, kv_cache, cache_lengths, first, rows):
    _, heads, depth = queries.shape
    live = kv_cache.shape[1]
    skip = first // PER_STEP
    return pl.pallas_call(
        lambda *refs: attend_kernel(first, *refs),
        grid_spec=pltpu.PrefetchScalarGridSpec(
            num_scalar_prefetch=1,
            grid=(rows // PER_STEP,),
            in_specs=[
                pl.BlockSpec((PER_STEP, depth, heads), lambda i, n: (i + skip, 0, 0)),
                pl.BlockSpec((PER_STEP, depth, live), lambda i, n: (i + skip, 0, 0)),
            ],
            out_specs=pl.BlockSpec((16, PER_STEP, heads // 16, LATENT), lambda i, n: (0, i, 0, 0)),
        ),
        out_shape=jax.ShapeDtypeStruct((16, rows, heads // 16, LATENT), BF),
        name="attend",
    )(cache_lengths, jnp.swapaxes(queries, 1, 2), jnp.swapaxes(kv_cache, 1, 2))


def project_kernel(steps, left_in, right_in, own_ref, other_ref, *outs):
    depth = own_ref.shape[0]

    def run(rows_ref, keep_ref, send_ref):
        result = jnp.dot(rows_ref[:, :depth], own_ref[...], preferred_element_type=F32)
        result += jnp.dot(rows_ref[:, depth:], other_ref[...], preferred_element_type=F32)
        half = result.shape[0] // 2
        keep_ref[...] = result[:half].astype(BF)
        send_ref[...] = result[half:].astype(BF)

    @pl.when(pl.program_id(0) < steps)
    def _():
        run(left_in, *outs[:2])

    @pl.when(pl.program_id(0) >= steps)
    def _():
        run(right_in, *outs[2:])


def project(left_in, right_in, own, other):
    rows, depth = left_in.shape
    width = own.shape[1]
    block = 1792
    steps = width // 2 // block
    whole = pl.BlockSpec((rows, depth), lambda i: (0, 0))
    matrix = pl.BlockSpec((depth // 2, block), lambda i: (0, i))
    shape = jax.ShapeDtypeStruct((rows // 2, width // 2), BF)
    left_out = pl.BlockSpec((rows // 2, block), lambda i: (0, jnp.minimum(i, steps - 1)))
    right_out = pl.BlockSpec((rows // 2, block), lambda i: (0, jnp.maximum(i - steps, 0)))
    return pl.pallas_call(
        lambda *refs: project_kernel(steps, *refs),
        grid=(2 * steps,),
        in_specs=[whole, whole, matrix, matrix],
        out_specs=[left_out, left_out, right_out, right_out],
        out_shape=[shape] * 4,
        name="project",
    )(left_in, right_in, own, other)


BLOCK = 1024
AHEAD = 3


def experts_kernel(
    number_ref, xa, xb, gate_own, up_own, gate_other, up_other, down_own, down_other,
    out_a, out_b, rows_ref, into, back, acc, hidden, row_sems, into_sems, back_sems,
):
    rows = xa.shape[0]
    steps, _, _, units = into.shape
    width = steps * BLOCK
    inward = (gate_own, up_own, gate_other, up_other)
    outward = (down_own, down_other)

    def span(step):
        return pl.ds(pl.multiple_of(step * BLOCK, BLOCK), BLOCK)

    def into_copies(step):
        return [
            pltpu.make_async_copy(m.at[0, span(step)], into.at[step, at], into_sems.at[step, at])
            for at, m in enumerate(inward)
        ]

    def back_copies(step):
        return [
            pltpu.make_async_copy(
                m.at[0, :, span(step)], back.at[step, at], back_sems.at[step, at]
            )
            for at, m in enumerate(outward)
        ]

    def start(copies):
        for copy in copies:
            copy.start()

    def wait(copies):
        for copy in copies:
            copy.wait()

    row_copies = [
        pltpu.make_async_copy(xa, rows_ref.at[:rows], row_sems.at[0]),
        pltpu.make_async_copy(xb, rows_ref.at[rows:], row_sems.at[1]),
    ]
    start(row_copies)
    for step in range(AHEAD):
        start(into_copies(step))
    acc[...] = jnp.zeros_like(acc)
    wait(row_copies)

    def inward_step(step, carry):
        @pl.when(step + AHEAD < steps)
        def _():
            start(into_copies(step + AHEAD))

        @pl.when(step + AHEAD >= steps)
        def _():
            start(back_copies(step + AHEAD - steps))

        wait(into_copies(step))
        block = rows_ref[:, span(step)]
        for at in range(4):
            acc[at] += jnp.dot(block, into[step, at], preferred_element_type=F32)
        return carry

    lax.fori_loop(0, steps, inward_step, 0)
    table = rows_ref[:, width:].astype(F32)
    ids, codes = table[:, :8], table[:, 8:16]
    weights = 2.5 * codes / jnp.sum(codes, axis=1, keepdims=True)
    for at in range(2):
        gate, up = acc[2 * at], acc[2 * at + 1]
        named = ids == number_ref[at].astype(F32)
        share = jnp.sum(jnp.where(named, weights, 0.0), axis=1, keepdims=True)
        value = gate / (1.0 + jnp.exp(-gate)) * up * share
        hidden[:, at * units : (at + 1) * units] = value.astype(BF)

    def outward_step(step, carry):
        @pl.when(step + AHEAD < steps)
        def _():
            start(back_copies(step + AHEAD))

        wait(back_copies(step))
        result = jnp.dot(hidden[:, :units], back[step, 0], preferred_element_type=F32)
        result += jnp.dot(hidden[:, units:], back[step, 1], preferred_element_type=F32)
        out_a[:, span(step)] = result[:rows].astype(BF)
        out_b[:, span(step)] = result[rows:].astype(BF)
        return carry

    lax.fori_loop(0, steps, outward_step, 0)


def experts(numbers, xa, xb, weights, width):
    rows = xa.shape[0]
    units = weights[0].shape[2]
    steps = width // BLOCK
    shape = jax.ShapeDtypeStruct((rows, width), BF)
    vmem = pl.BlockSpec(memory_space=pltpu.VMEM)
    far = pl.BlockSpec(memory_space=pl.ANY)
    return pl.pallas_call(
        experts_kernel,
        in_specs=[pl.BlockSpec(memory_space=pltpu.SMEM)] + [far] * 8,
        out_specs=[vmem, vmem],
        out_shape=[shape, shape],
        scratch_shapes=[
            pltpu.VMEM((2 * rows, xa.shape[1]), BF),
            pltpu.VMEM((steps, 4, BLOCK, units), BF),
            pltpu.VMEM((steps, 2, units, BLOCK), BF),
            pltpu.VMEM((4, 2 * rows, units), F32),
            pltpu.VMEM((2 * rows, 2 * units), BF),
            pltpu.SemaphoreType.DMA((2,)),
            pltpu.SemaphoreType.DMA((steps, 4)),
            pltpu.SemaphoreType.DMA((steps, 2)),
        ],
        compiler_params=pltpu.CompilerParams(vmem_limit_bytes=32 << 20),
        name="experts",
    )(numbers, xa, xb, *weights)


def ring_offset(bits, core):
    low, high = bits % 2, bits // 2
    first = jnp.where(core == 0, 1, 3)
    second = jnp.where(core == 0, 3, 1)
    return (low * first) ^ (high * second)


def plane_order(rows, here, core, y_first):
    count = rows // 16
    at = jnp.arange(rows, dtype=jnp.int32)
    block = at // count
    major, minor = block // 4, block % 4
    y = (here // 4) ^ ring_offset(major if y_first else minor, core)
    x = (here % 4) ^ ring_offset(minor if y_first else major, core)
    part = count // PARTS
    request = at % count
    source = (request // part) * (16 * part) + (y * 4 + x) * part + request % part
    return (source[:, None] == jnp.arange(rows, dtype=jnp.int32)[None, :]).astype(BF)


def halves(value):
    half = value.shape[0] // 2
    return value[:half], value[half:]


def add(one, two):
    return (one.astype(F32) + two.astype(F32)).astype(BF)


def fold(value, axis, step):
    keep, send = halves(value)
    got = swap(send, axis, step)
    return (keep.astype(F32) + got.astype(F32)).astype(BF)


def grow(value, axis, step):
    return jnp.concatenate([value, swap(value, axis, step)], axis=0)


def run_rows(
    hidden_rows,
    queries,
    kv_cache,
    cache_lengths,
    value_lift,
    out_weight,
    expert_ids,
    weight_codes,
    w_gate,
    w_up,
    w_down,
):
    device = lax.axis_index("dev")
    core = device % 2
    here = device // 2
    rows, width = hidden_rows.shape

    swapped = []
    for matrix in (value_lift, out_weight, w_gate, w_up, w_down):
        swapped.append(other_core(matrix))
    lift_other, out_other, gate_other, up_other, down_other = swapped

    same_core = [[c + 2 * i for i in range(16)] for c in range(2)]
    moved = []
    for at in range(PARTS):
        heads_out = attend(queries, kv_cache, cache_lengths, at * (rows // PARTS), rows // PARTS)
        arrived = lax.all_to_all(
            heads_out, "dev", split_axis=0, concat_axis=0, tiled=True,
            axis_index_groups=same_core,
        )
        moved.append(arrived.reshape(-1, arrived.shape[2], LATENT))
    all_rows = 16 * rows

    def lifted(part, lift):
        return jnp.einsum("rhl,hlv->rhv", part, lift, preferred_element_type=F32).astype(BF)

    def head_pair(arrived):
        own = lax.dynamic_slice_in_dim(arrived, 4 * core, 4, 1)
        other = lax.dynamic_slice_in_dim(arrived, 4 * (1 - core), 4, 1)
        return jnp.concatenate(
            [lifted(own, value_lift), lifted(other, lift_other)], axis=1
        ).reshape(all_rows // PARTS, -1)

    head_values = jnp.concatenate([head_pair(arrived) for arrived in moved], axis=0)

    def ordered(y_first):
        order = plane_order(all_rows, here, core, y_first)
        return jnp.dot(order, head_values, preferred_element_type=F32).astype(BF)

    left_keep, left_send, right_keep, right_send = project(
        ordered(True),
        ordered(False),
        out_weight.reshape(-1, width),
        out_other.reshape(-1, width),
    )
    left = add(left_keep, swap(left_send, Y, 1))
    right = add(right_keep, swap(right_send, X, 1))
    for axis_left, axis_right, step in ((Y, X, 0), (X, Y, 1), (X, Y, 0)):
        left = fold(left, axis_left, step)
        right = fold(right, axis_right, step)
    attention = jnp.concatenate([left, right], axis=1).astype(F32)
    residual = hidden_rows.astype(F32) + attention
    normed = (
        residual * lax.rsqrt(jnp.mean(residual * residual, axis=1, keepdims=True) + 1e-06)
    ).astype(BF)

    routing = jnp.concatenate([expert_ids, weight_codes], axis=1).astype(BF)
    routing = jnp.pad(routing, ((0, 0), (0, 128 - routing.shape[1])))
    mine = jnp.concatenate([normed, routing], axis=1)
    from_one, from_two, from_three = [onward(mine, Z, hops) for hops in (1, 2, 3)]
    first = jnp.concatenate([mine, from_one], axis=0)
    second = jnp.concatenate([from_two, from_three], axis=0)
    for step in range(2):
        first = grow(first, X, step)
        second = grow(second, Y, step)

    numbers = jnp.stack([device, device ^ 1]).astype(jnp.int32)
    weights = (w_gate, w_up, gate_other, up_other, w_down, down_other)

    def both(pair, hops):
        moved_on = []
        for at, axis in enumerate((Y, X)):
            moved_on.append(onward(pair[at], axis, hops))
        return moved_on

    held = [(first, second)]
    held.append(both(held[0], 1))
    from_ahead = both(held[0], 3)
    held.append(both(held[1], 1))
    held.append(from_ahead)
    done = []
    for hop in range(4):
        done.append(experts(numbers, *held[hop], weights, width))
    near = both(done[1], 3)
    far = both(done[2], 1)
    far = [add(done[3][at], far[at]) for at in range(2)]
    far = both(far, 1)
    one, two = [
        (done[0][at].astype(F32) + near[at].astype(F32) + far[at].astype(F32)).astype(BF)
        for at in range(2)
    ]
    for step in (1, 0):
        one = fold(one, X, step)
        two = fold(two, Y, step)
    keep, to_one = halves(one)
    to_two, to_three = halves(two)
    combined = keep.astype(F32)
    for part, hops in ((to_one, 3), (to_two, 2), (to_three, 1)):
        combined += onward(part, Z, hops).astype(F32)
    return (residual + combined).astype(BF)


def solution(mesh):
    both = P(ALL, None)
    in_specs = (
        both,
        P(ALL, None, None),
        P(ALL, None, None),
        P(ALL),
        P("dev", None, None),
        P("dev", None, None),
        both,
        both,
        P("dev", None, "grp"),
        P("dev", None, "grp"),
        P("dev", "grp", None),
    )
    return jax.shard_map(run_rows, mesh=mesh, in_specs=in_specs, out_specs=both, check_vma=False)
```

```python
import jax
import jax.numpy as jnp
from jax import lax
from jax.experimental import pallas as pl
from jax.experimental.pallas import tpu as pltpu
from jax.sharding import PartitionSpec as P


LATENT = 512
SCALE = 192.0 ** (-0.5)
ALL = ("grp", "dev")
BF = jnp.bfloat16
F32 = jnp.float32


def place(i):
    return [i // 32, (i // 8) % 4, (i // 2) % 4, i % 2]


def number(at):
    return ((at[0] * 4 + at[1]) * 4 + at[2]) * 2 + at[3]


def core_pairs():
    return [(i, i ^ 1) for i in range(128)]


def ring_pairs(axis, step):
    pairs = []
    for i in range(128):
        at = place(i)
        flip = (1, 3) if at[3] == 0 else (3, 1)
        at[axis] ^= flip[step]
        pairs.append((i, number(at)))
    return pairs


def ring_next(axis, hops=1):
    pairs = []
    for i in range(128):
        at = place(i)
        at[axis] = (at[axis] + (hops if at[3] == 0 else 4 - hops)) % 4
        pairs.append((i, number(at)))
    return pairs


Z, Y, X = 0, 1, 2


def swap(value, axis, step):
    return lax.ppermute(value, ALL, ring_pairs(axis, step))


def onward(value, axis, hops=1):
    return lax.ppermute(value, ALL, ring_next(axis, hops))


def other_core(value):
    return lax.ppermute(value, ALL, core_pairs())


PER_STEP = 2
PARTS = 1


def attend_kernel(first, length_ref, q_ref, kv_ref, out_ref):
    for j in range(PER_STEP):
        kv = kv_ref[j]
        logits = lax.dot_general(
            q_ref[j], kv, (((0,), (0,)), ((), ())), preferred_element_type=F32
        ) * SCALE
        live = lax.broadcasted_iota(jnp.int32, logits.shape, 1) < length_ref[
            first + pl.program_id(0) * PER_STEP + j
        ]
        logits = jnp.where(live, logits, -jnp.inf)
        exponent = jnp.exp(logits - jnp.max(logits, axis=1, keepdims=True))
        soft = (exponent / jnp.sum(exponent, axis=1, keepdims=True)).astype(BF)
        result = lax.dot_general(
            soft, kv[:LATENT], (((1,), (1,)), ((), ())), preferred_element_type=F32
        )
        out_ref[:, j] = result.astype(BF).reshape(out_ref.shape[0], out_ref.shape[2], LATENT)


def attend(queries, kv_cache, cache_lengths, first, rows):
    _, heads, depth = queries.shape
    live = kv_cache.shape[1]
    skip = first // PER_STEP
    return pl.pallas_call(
        lambda *refs: attend_kernel(first, *refs),
        grid_spec=pltpu.PrefetchScalarGridSpec(
            num_scalar_prefetch=1,
            grid=(rows // PER_STEP,),
            in_specs=[
                pl.BlockSpec((PER_STEP, depth, heads), lambda i, n: (i + skip, 0, 0)),
                pl.BlockSpec((PER_STEP, depth, live), lambda i, n: (i + skip, 0, 0)),
            ],
            out_specs=pl.BlockSpec((16, PER_STEP, heads // 16, LATENT), lambda i, n: (0, i, 0, 0)),
        ),
        out_shape=jax.ShapeDtypeStruct((16, rows, heads // 16, LATENT), BF),
        name="attend",
    )(cache_lengths, jnp.swapaxes(queries, 1, 2), jnp.swapaxes(kv_cache, 1, 2))


def project_kernel(steps, left_in, right_in, own_ref, other_ref, *outs):
    depth = own_ref.shape[0]

    def run(rows_ref, keep_ref, send_ref):
        result = jnp.dot(rows_ref[:, :depth], own_ref[...], preferred_element_type=F32)
        result += jnp.dot(rows_ref[:, depth:], other_ref[...], preferred_element_type=F32)
        half = result.shape[0] // 2
        keep_ref[...] = result[:half].astype(BF)
        send_ref[...] = result[half:].astype(BF)

    @pl.when(pl.program_id(0) < steps)
    def _():
        run(left_in, *outs[:2])

    @pl.when(pl.program_id(0) >= steps)
    def _():
        run(right_in, *outs[2:])


def project(left_in, right_in, own, other):
    rows, depth = left_in.shape
    width = own.shape[1]
    block = 1792
    steps = width // 2 // block
    whole = pl.BlockSpec((rows, depth), lambda i: (0, 0))
    matrix = pl.BlockSpec((depth // 2, block), lambda i: (0, i))
    shape = jax.ShapeDtypeStruct((rows // 2, width // 2), BF)
    left_out = pl.BlockSpec((rows // 2, block), lambda i: (0, jnp.minimum(i, steps - 1)))
    right_out = pl.BlockSpec((rows // 2, block), lambda i: (0, jnp.maximum(i - steps, 0)))
    return pl.pallas_call(
        lambda *refs: project_kernel(steps, *refs),
        grid=(2 * steps,),
        in_specs=[whole, whole, matrix, matrix],
        out_specs=[left_out, left_out, right_out, right_out],
        out_shape=[shape] * 4,
        name="project",
    )(left_in, right_in, own, other)


BLOCK = 1024
AHEAD = 3


def experts_kernel(
    number_ref, xa, xb, gate_own, up_own, gate_other, up_other, down_own, down_other,
    out_a, out_b, rows_ref, into, back, acc, hidden, row_sems, into_sems, back_sems,
):
    rows = xa.shape[0]
    steps, _, _, units = into.shape
    width = steps * BLOCK
    inward = (gate_own, up_own, gate_other, up_other)
    outward = (down_own, down_other)

    def span(step):
        return pl.ds(pl.multiple_of(step * BLOCK, BLOCK), BLOCK)

    def into_copies(step):
        return [
            pltpu.make_async_copy(m.at[0, span(step)], into.at[step, at], into_sems.at[step, at])
            for at, m in enumerate(inward)
        ]

    def back_copies(step):
        return [
            pltpu.make_async_copy(
                m.at[0, :, span(step)], back.at[step, at], back_sems.at[step, at]
            )
            for at, m in enumerate(outward)
        ]

    def start(copies):
        for copy in copies:
            copy.start()

    def wait(copies):
        for copy in copies:
            copy.wait()

    row_copies = [
        pltpu.make_async_copy(xa, rows_ref.at[:rows], row_sems.at[0]),
        pltpu.make_async_copy(xb, rows_ref.at[rows:], row_sems.at[1]),
    ]
    start(row_copies)
    for step in range(AHEAD):
        start(into_copies(step))
    acc[...] = jnp.zeros_like(acc)
    wait(row_copies)

    def inward_step(step, carry):
        @pl.when(step + AHEAD < steps)
        def _():
            start(into_copies(step + AHEAD))

        @pl.when(step + AHEAD >= steps)
        def _():
            start(back_copies(step + AHEAD - steps))

        wait(into_copies(step))
        block = rows_ref[:, span(step)]
        for at in range(4):
            acc[at] += jnp.dot(block, into[step, at], preferred_element_type=F32)
        return carry

    lax.fori_loop(0, steps, inward_step, 0)
    table = rows_ref[:, width:].astype(F32)
    ids, codes = table[:, :8], table[:, 8:16]
    weights = 2.5 * codes / jnp.sum(codes, axis=1, keepdims=True)
    for at in range(2):
        gate, up = acc[2 * at], acc[2 * at + 1]
        named = ids == number_ref[at].astype(F32)
        share = jnp.sum(jnp.where(named, weights, 0.0), axis=1, keepdims=True)
        value = gate / (1.0 + jnp.exp(-gate)) * up * share
        hidden[:, at * units : (at + 1) * units] = value.astype(BF)

    def outward_step(step, carry):
        @pl.when(step + AHEAD < steps)
        def _():
            start(back_copies(step + AHEAD))

        wait(back_copies(step))
        result = jnp.dot(hidden[:, :units], back[step, 0], preferred_element_type=F32)
        result += jnp.dot(hidden[:, units:], back[step, 1], preferred_element_type=F32)
        out_a[:, span(step)] = result[:rows].astype(BF)
        out_b[:, span(step)] = result[rows:].astype(BF)
        return carry

    lax.fori_loop(0, steps, outward_step, 0)


def experts(numbers, xa, xb, weights, width):
    rows = xa.shape[0]
    units = weights[0].shape[2]
    steps = width // BLOCK
    shape = jax.ShapeDtypeStruct((rows, width), BF)
    vmem = pl.BlockSpec(memory_space=pltpu.VMEM)
    far = pl.BlockSpec(memory_space=pl.ANY)
    return pl.pallas_call(
        experts_kernel,
        in_specs=[pl.BlockSpec(memory_space=pltpu.SMEM)] + [far] * 8,
        out_specs=[vmem, vmem],
        out_shape=[shape, shape],
        scratch_shapes=[
            pltpu.VMEM((2 * rows, xa.shape[1]), BF),
            pltpu.VMEM((steps, 4, BLOCK, units), BF),
            pltpu.VMEM((steps, 2, units, BLOCK), BF),
            pltpu.VMEM((4, 2 * rows, units), F32),
            pltpu.VMEM((2 * rows, 2 * units), BF),
            pltpu.SemaphoreType.DMA((2,)),
            pltpu.SemaphoreType.DMA((steps, 4)),
            pltpu.SemaphoreType.DMA((steps, 2)),
        ],
        compiler_params=pltpu.CompilerParams(vmem_limit_bytes=32 << 20),
        name="experts",
    )(numbers, xa, xb, *weights)


def ring_offset(bits, core):
    low, high = bits % 2, bits // 2
    first = jnp.where(core == 0, 1, 3)
    second = jnp.where(core == 0, 3, 1)
    return (low * first) ^ (high * second)


def plane_order(rows, here, core, y_first):
    count = rows // 16
    at = jnp.arange(rows, dtype=jnp.int32)
    block = at // count
    major, minor = block // 4, block % 4
    y = (here // 4) ^ ring_offset(major if y_first else minor, core)
    x = (here % 4) ^ ring_offset(minor if y_first else major, core)
    part = count // PARTS
    request = at % count
    source = (request // part) * (16 * part) + (y * 4 + x) * part + request % part
    return (source[:, None] == jnp.arange(rows, dtype=jnp.int32)[None, :]).astype(BF)


def halves(value):
    half = value.shape[0] // 2
    return value[:half], value[half:]


def add(one, two):
    return (one.astype(F32) + two.astype(F32)).astype(BF)


def fold(value, axis, step):
    keep, send = halves(value)
    got = swap(send, axis, step)
    return (keep.astype(F32) + got.astype(F32)).astype(BF)


def grow(value, axis, step):
    return jnp.concatenate([value, swap(value, axis, step)], axis=0)


def run_rows(
    hidden_rows,
    queries,
    kv_cache,
    cache_lengths,
    value_lift,
    out_weight,
    expert_ids,
    weight_codes,
    w_gate,
    w_up,
    w_down,
):
    device = lax.axis_index("dev")
    core = device % 2
    here = device // 2
    rows, width = hidden_rows.shape

    swapped = []
    for matrix in (value_lift, out_weight, w_gate, w_up, w_down):
        swapped.append(other_core(matrix))
    lift_other, out_other, gate_other, up_other, down_other = swapped

    same_core = [[c + 2 * i for i in range(16)] for c in range(2)]
    moved = []
    for at in range(PARTS):
        heads_out = attend(queries, kv_cache, cache_lengths, at * (rows // PARTS), rows // PARTS)
        arrived = lax.all_to_all(
            heads_out, "dev", split_axis=0, concat_axis=0, tiled=True,
            axis_index_groups=same_core,
        )
        moved.append(arrived.reshape(-1, arrived.shape[2], LATENT))
    all_rows = 16 * rows

    def lifted(part, lift):
        return jnp.einsum("rhl,hlv->rhv", part, lift, preferred_element_type=F32).astype(BF)

    def head_pair(arrived):
        own = lax.dynamic_slice_in_dim(arrived, 4 * core, 4, 1)
        other = lax.dynamic_slice_in_dim(arrived, 4 * (1 - core), 4, 1)
        return jnp.concatenate(
            [lifted(own, value_lift), lifted(other, lift_other)], axis=1
        ).reshape(all_rows // PARTS, -1)

    head_values = jnp.concatenate([head_pair(arrived) for arrived in moved], axis=0)

    def ordered(y_first):
        order = plane_order(all_rows, here, core, y_first)
        return jnp.dot(order, head_values, preferred_element_type=F32).astype(BF)

    left_keep, left_send, right_keep, right_send = project(
        ordered(True),
        ordered(False),
        out_weight.reshape(-1, width),
        out_other.reshape(-1, width),
    )
    left = add(left_keep, swap(left_send, Y, 1))
    right = add(right_keep, swap(right_send, X, 1))
    for axis_left, axis_right, step in ((Y, X, 0), (X, Y, 1), (X, Y, 0)):
        left = fold(left, axis_left, step)
        right = fold(right, axis_right, step)
    attention = jnp.concatenate([left, right], axis=1).astype(F32)
    residual = hidden_rows.astype(F32) + attention
    normed = (
        residual * lax.rsqrt(jnp.mean(residual * residual, axis=1, keepdims=True) + 1e-06)
    ).astype(BF)

    routing = jnp.concatenate([expert_ids, weight_codes], axis=1).astype(BF)
    routing = jnp.pad(routing, ((0, 0), (0, 128 - routing.shape[1])))
    mine = jnp.concatenate([normed, routing], axis=1)
    from_one, from_two, from_three = [onward(mine, Z, hops) for hops in (1, 2, 3)]
    first = jnp.concatenate([mine, from_one], axis=0)
    second = jnp.concatenate([from_two, from_three], axis=0)
    for step in range(2):
        first = grow(first, X, step)
        second = grow(second, Y, step)

    numbers = jnp.stack([device, device ^ 1]).astype(jnp.int32)
    weights = (w_gate, w_up, gate_other, up_other, w_down, down_other)
    held = [(first, second)]
    for _ in range(1, 4):
        one = onward(held[-1][0], Y)
        two = onward(held[-1][1], X)
        held.append((one, two))
    done = []
    for hop in range(4):
        done.append(experts(numbers, *held[hop], weights, width))
    one, two = done[1]
    for hop in range(1, 4):
        one = onward(one, Y)
        two = onward(two, X)
        one = add(one, done[(hop + 1) % 4][0])
        two = add(two, done[(hop + 1) % 4][1])
    for step in (1, 0):
        one = fold(one, X, step)
        two = fold(two, Y, step)
    keep, to_one = halves(one)
    to_two, to_three = halves(two)
    combined = keep.astype(F32)
    for part, hops in ((to_one, 3), (to_two, 2), (to_three, 1)):
        combined += onward(part, Z, hops).astype(F32)
    return (residual + combined).astype(BF)


def solution(mesh):
    both = P(ALL, None)
    in_specs = (
        both,
        P(ALL, None, None),
        P(ALL, None, None),
        P(ALL),
        P("dev", None, None),
        P("dev", None, None),
        both,
        both,
        P("dev", None, "grp"),
        P("dev", None, "grp"),
        P("dev", "grp", None),
    )
    return jax.shard_map(run_rows, mesh=mesh, in_specs=in_specs, out_specs=both, check_vma=False)
```
